1024 devices in a mesh: enc: 16 (over y, x), seq: 64 (over z, core).
Axes of the slice: x: 4, y: 4, z: 32, core: 2. Of those that a mesh axis runs over, the one named last changes fastest.
Arguments:
- qkv: bfloat16 [64, 4096, 3840], P('enc', 'seq'), may hold values from -6 to 6
- resid: bfloat16 [64, 4096, 1280], P('enc', 'seq'), may hold values from -6 to 6
- block_count: int32 [16, 64], P('enc', 'seq'), may hold values from 2 to 4, as said below
- send_count: int32 [16, 64], P('enc', 'seq'), may hold values from 0 to 1, as said below
- send_slot: int32 [16, 3072], P('enc', 'seq'), may hold values from 0 to 63, as said below
- lm_row: int32 [16, 4096], P('enc', 'seq'), may hold values from -1 to 47, as said below
- out_weight: bfloat16 [1280, 1280], replicated, may hold values from -0.15625 to 0.15625
- out_bias: bfloat16 [1280], replicated, may hold values from -3 to 3
- norm_gain: bfloat16 [1280], replicated, may hold values from 0.25 to 1.75
Outputs:
- lm_tokens: bfloat16 [16, 3072, 5120], P('enc', 'seq')
The draws below stay inside these ranges and needn't reach their ends.
Inputs may be any that keep to these rules, and one draw needn't show every extreme that they name: send_count is at most 1; a device's live slots come first. block_count[e, g] = 3 + send_count[e, g] - send_count[(e - 1) mod 16, g]. `send_slot`: values of one device are distinct; with o = (s - g) mod 64 and finv(o) = 2 * o for o < 32, else 2 * (o - 32) + 1, the device at seq index g uses slot s + k exactly when k * 64 + finv(o) < 48. `lm_row`: at seq index s, with o and finv as for send_slot, arriving slot g + k holds -1 exactly when k * 64 + finv((s - g) mod 64) >= 48; the other slots hold each of 0 to 47 once.
All inputs are finite; a program needn't handle non-finite values.
Results may differ from the reference program's by a relative error of at most 0.0036.
Values may be sent and summed in bfloat16 or wider, within the bound.
A program may use at most 32 MiB of HBM per device.

```python
import math
import jax
import jax.numpy as jnp
from jax import lax

D = 1280
HEADS = 16
WIN = 64
SPARE = 1
BLOCKS = 3
SLOTS = 4
ROWS_OUT = 48
CAP = 1
N_ENC = 16
N_SEQ = 64


def lent_table(key):
    lent_count = jax.random.randint(jax.random.fold_in(key, 7), (N_ENC, N_SEQ), 0, SPARE + 1)
    lent_count = lent_count.at[0, 0].set(SPARE).at[1, 0].set(0).at[N_ENC - 1, 0].set(0)
    return lent_count.astype(jnp.int32)


def draw_send_count(key, part):
    return lent_table(key)


def draw_block_count(key, part):
    lent_count = lent_table(key)
    return (BLOCKS + lent_count - jnp.roll(lent_count, 1, axis=0)).astype(jnp.int32)


def spread_offset(index_in):
    return index_in // 2 + index_in % 2 * (N_SEQ // 2)


def spread_inverse(offset):
    return jnp.where(offset < N_SEQ // 2, 2 * offset, 2 * (offset - N_SEQ // 2) + 1)


def draw_send_slot(key, part):
    row_ids = jnp.arange(ROWS_OUT, dtype=jnp.int32)
    scores = jax.random.randint(key, (N_ENC, N_SEQ, ROWS_OUT), 0, 1 << 20) * ROWS_OUT + row_ids
    ranks = jnp.argsort(scores, axis=-1).astype(jnp.int32)
    offset = spread_offset(ranks % N_SEQ)
    seq_ids = jnp.arange(N_SEQ, dtype=jnp.int32)[None, :, None]
    target = (seq_ids + offset) % N_SEQ
    return (target * CAP + ranks // N_SEQ).reshape(N_ENC, N_SEQ * ROWS_OUT).astype(jnp.int32)


def draw_lm_row(key, part):
    slot_total = N_SEQ * CAP
    slot_ids = jnp.arange(slot_total, dtype=jnp.int32)
    sender = slot_ids // CAP
    rank_k = slot_ids % CAP
    seq_ids = jnp.arange(N_SEQ, dtype=jnp.int32)[:, None]
    offset = (seq_ids - sender[None, :]) % N_SEQ
    filled = rank_k[None, :] * N_SEQ + spread_inverse(offset) < ROWS_OUT
    scores = jax.random.randint(key, (N_ENC, N_SEQ, slot_total), 0, 1 << 20) * slot_total + slot_ids
    scores = jnp.where(filled[None], scores, (1 << 20) * slot_total + slot_ids)
    position = jnp.argsort(jnp.argsort(scores, axis=-1), axis=-1).astype(jnp.int32)
    return jnp.where(filled[None], position, -1).reshape(N_ENC, N_SEQ * slot_total).astype(jnp.int32)


def draw_qkv(key, part):
    head_size = D // HEADS
    shape = (N_ENC * SLOTS, N_SEQ, WIN, 3, HEADS, head_size)
    values = jnp.clip(jax.random.normal(key, shape), -4.0, 4.0)
    return values.reshape(N_ENC * SLOTS, N_SEQ * WIN, 3 * D).astype(jnp.bfloat16)


def block_levels(own_key, extent, cuts, low, largest):
    def one(dim, parts):
        draws = jax.random.uniform(jax.random.fold_in(jax.random.fold_in(own_key, 6), dim), (parts,), jnp.float32, low / len(cuts), largest / len(cuts))
        return jnp.repeat(jnp.exp(draws), extent[dim] // parts).reshape((-1,) + (1,) * (len(extent) - dim - 1))

    level = one(*cuts[0])
    for cut in cuts[1:]:
        level = level * one(*cut)
    return level


def normal_values(key, dims, width, limit, cuts=(), kind=jnp.bfloat16):
    entries = jax.random.normal(key, dims, jnp.float32) * width
    if len(cuts) > 0:
        entries = block_levels(key, dims, cuts, -0.22, 0.18) * entries
    return jnp.clip(entries, min=-limit, max=limit).astype(kind)


def setup_inputs(seed: int = 0) -> dict:
    keys = jax.random.split(jax.random.key(seed), 10)
    return {
        "qkv": draw_qkv(jax.random.fold_in(keys[9], 71), 0),
        "resid": normal_values(keys[1], (N_ENC * SLOTS, N_SEQ * WIN, D), 1.0, 6.0, ((0, 16), (1, 64))),
        "block_count": draw_block_count(jax.random.fold_in(keys[9], 71), 0),
        "send_count": draw_send_count(jax.random.fold_in(keys[9], 71), 0),
        "send_slot": draw_send_slot(jax.random.fold_in(keys[9], 71), 0),
        "lm_row": draw_lm_row(jax.random.fold_in(keys[9], 71), 0),
        "out_weight": normal_values(keys[6], (D, D), D ** -0.5, 0.15625),
        "out_bias": normal_values(keys[7], (D,), 0.5, 3.0),
        "norm_gain": jnp.clip(1.0 + 0.15 * jax.random.normal(keys[8], (D,), jnp.float32), 0.25, 1.75).astype(jnp.bfloat16),
    }


def encode_blocks(qkv_blocks, resid_blocks, out_weight, out_bias, norm_gain):
    block_total = qkv_blocks.shape[0]
    window_len = qkv_blocks.shape[1]
    model_width = resid_blocks.shape[2]
    head_size = model_width // HEADS
    packed = qkv_blocks.astype(jnp.float32).reshape(block_total, window_len, 3, HEADS, head_size)
    queries = packed[:, :, 0]
    key_rows = packed[:, :, 1]
    value_rows = packed[:, :, 2]
    scores = jnp.einsum('bqhd,bkhd->bhqk', queries, key_rows) * (1.0 / math.sqrt(head_size))
    exp_scores = jnp.exp(scores - lax.optimization_barrier(jnp.max(scores, axis=-1, keepdims=True)))
    probabilities = (exp_scores / lax.optimization_barrier(jnp.sum(exp_scores, axis=-1, keepdims=True))).astype(jnp.bfloat16)
    attended = jnp.einsum('bhqk,bkhd->bqhd', probabilities.astype(jnp.float32), value_rows).astype(jnp.bfloat16)
    flat_rows = attended.reshape(block_total * window_len, model_width)
    hidden = jnp.dot(flat_rows, out_weight, preferred_element_type=jnp.float32)
    hidden = hidden + out_bias.astype(jnp.float32) + resid_blocks.reshape(block_total * window_len, model_width).astype(jnp.float32)
    inv_rms = lax.rsqrt(lax.optimization_barrier(jnp.mean(hidden * hidden, axis=-1, keepdims=True)) + 1e-06)
    normed = (hidden * inv_rms * norm_gain.astype(jnp.float32)).astype(jnp.bfloat16)
    return normed.reshape(block_total, window_len // 4, 4 * model_width)

def reference(qkv, resid, block_count, send_count, send_slot, lm_row, out_weight, out_bias, norm_gain):
    qkv_dev = qkv.reshape(N_ENC, SLOTS * N_SEQ, WIN, 3 * D)
    resid_dev = resid.reshape(N_ENC, SLOTS * N_SEQ, WIN, D)

    def per_enc(pair):
        return encode_blocks(pair[0], pair[1], out_weight, out_bias, norm_gain)
    merged_all = lax.map(per_enc, (qkv_dev, resid_dev))
    merged_all = merged_all.reshape(N_ENC, SLOTS, N_SEQ, WIN // 4, 4 * D)
    enc_ids = jnp.arange(N_ENC, dtype=jnp.int32)[:, None, None]
    seq_ids = jnp.arange(N_SEQ, dtype=jnp.int32)[None, :, None]
    work_ids = jnp.arange(BLOCKS, dtype=jnp.int32)[None, None, :]
    kept_blocks = (block_count - send_count)[:, :, None]
    prev_count = jnp.roll(block_count, 1, axis=0)[:, :, None]
    prev_send = jnp.roll(send_count, 1, axis=0)[:, :, None]
    own_block = work_ids < kept_blocks
    src_enc = jnp.where(own_block, enc_ids, (enc_ids - 1) % N_ENC)
    src_slot = jnp.where(own_block, work_ids, prev_count - prev_send + work_ids - kept_blocks)
    seq_full = jnp.broadcast_to(seq_ids, src_slot.shape)
    work_rows = merged_all[src_enc, src_slot, seq_full]
    work_rows = work_rows.reshape(N_ENC, N_SEQ, ROWS_OUT, 4 * D)
    slot_value = send_slot.reshape(N_ENC, N_SEQ, ROWS_OUT)
    dest_seq = slot_value // CAP
    arrive_slot = seq_ids * CAP + slot_value % CAP
    flat_index = (dest_seq * (N_SEQ * CAP) + arrive_slot).reshape(N_ENC, N_SEQ * ROWS_OUT)
    place_row = jnp.take_along_axis(lm_row, flat_index, axis=1).reshape(N_ENC, N_SEQ, ROWS_OUT)
    final_row = dest_seq * ROWS_OUT + place_row
    lm_tokens = jnp.zeros((N_ENC, N_SEQ * ROWS_OUT, 4 * D), jnp.bfloat16)
    lm_tokens = lm_tokens.at[jnp.broadcast_to(enc_ids, final_row.shape), final_row].set(work_rows)
    return lm_tokens
```

```python
import functools
import math

import jax
import jax.numpy as jnp
from jax import lax
from jax.experimental import pallas as pl
from jax.experimental.pallas import tpu as pltpu
from jax.sharding import PartitionSpec as P

MESH = pl.DeviceIdType.MESH
D = 1280
HALF = 640
HEAD = 80
WIN = 64
SEQ = 64
ENC = 16
TOK = 48
JUMP = 8
MOVED = (32, 33, 34)

UP = list(range(1, 24)) + list(MOVED)
DOWN = [o - 64 for o in range(55, 31, -1) if o not in MOVED]
OFFSETS = [0] + UP + DOWN


def full_jumps(offset):
    return (abs(offset) - 1) // JUMP if offset else 0


def jump_groups():
    groups = []
    i = 1
    while i < TOK:
        sign = 1 if OFFSETS[i] > 0 else -1
        jumps = full_jumps(OFFSETS[i])
        k = i
        while k < TOK and OFFSETS[k] * sign > 0 and full_jumps(OFFSETS[k]) == jumps:
            k += 1
        if jumps:
            groups.append((sign, jumps, i, k))
        i = k
    return groups


GROUPS = jump_groups()
ROUNDS = max(g[1] for g in GROUPS)


def last_offset(offset):
    sign = 1 if offset > 0 else -1
    return offset - sign * JUMP * full_jumps(offset)


PARTNERS = sorted(
    {last_offset(o) for o in OFFSETS if o} | {sign * JUMP for sign, _, _, _ in GROUPS}
)


def send_order():
    up = [i for i, g in enumerate(GROUPS) if g[0] > 0]
    down = [i for i, g in enumerate(GROUPS) if g[0] < 0]

    def far_first(ids):
        return sorted(ids, key=lambda i: (-GROUPS[i][1], -i))

    def weave(a, b):
        out = []
        for i in range(max(len(a), len(b))):
            out += b[i : i + 1] + a[i : i + 1]
        return out

    order = weave([("jump", i, 1) for i in far_first(up)], [("jump", i, 1) for i in far_first(down)])
    for turn in range(2, ROUNDS + 2):
        lanes = []
        for ids in (up, down):
            lane = []
            for i in far_first(ids):
                _, jumps, first, end = GROUPS[i]
                if jumps >= turn:
                    lane.append(("jump", i, turn))
                elif jumps == turn - 1:
                    lane += [("last", t) for t in range(end - 1, first - 1, -1)]
            lanes.append(lane)
        order += weave(*lanes)
        if turn == 2:
            order += [("last", t) for t in range(1, TOK) if full_jumps(OFFSETS[t]) == 0]
    return order


ORDER = send_order()


def place_offset(place):
    n_up = len(UP)
    return jnp.where(place < 24, place, jnp.where(place <= n_up, place + 8, 82 - place))


def encode_kernel(
    qkv_hbm,
    resid_hbm,
    count_ref,
    lent_ref,
    slot_ref,
    weight_hbm,
    bias_ref,
    gain_ref,
    out_hbm,
    qkv,
    resid,
    weight,
    att,
    lend,
    normed,
    outgoing,
    relay,
    load_sem,
    lend_sem,
    jump_send,
    jump_recv,
    last_send,
    last_recv,
    own_sem,
):
    me = lax.axis_index("seq")
    enc = lax.axis_index("enc")

    def along_seq(offset):
        return (enc, lax.rem(me + (offset % SEQ), SEQ))

    next_enc = (lax.rem(enc + 1, ENC), me)
    prev_enc = (lax.rem(enc + ENC - 1, ENC), me)

    barrier = pltpu.get_barrier_semaphore()
    for offset in PARTNERS:
        pl.semaphore_signal(barrier, inc=1, device_id=along_seq(-offset), device_id_type=MESH)
    pl.semaphore_signal(barrier, inc=1, device_id=prev_enc, device_id_type=MESH)

    loads = [
        pltpu.make_async_copy(qkv_hbm, qkv, load_sem.at[0]),
        pltpu.make_async_copy(weight_hbm, weight, load_sem.at[1]),
        pltpu.make_async_copy(resid_hbm, resid, load_sem.at[2]),
    ]
    for copy in loads:
        copy.start()

    live = count_ref[0, 0]
    kept = live - lent_ref[0, 0]
    last_live = jnp.clip(live - 1, 0, 3)
    bias = bias_ref[...].astype(jnp.float32)
    gain = gain_ref[...].astype(jnp.float32)

    col = lax.broadcasted_iota(jnp.int32, (1, 4 * WIN), 1)
    row48 = lax.broadcasted_iota(jnp.int32, (TOK, 4 * WIN), 0)
    col48 = lax.broadcasted_iota(jnp.int32, (TOK, 4 * WIN), 1)
    work_row = jnp.where(col48 < 3 * WIN, col48 // 4, (col48 - WIN) // 4)
    spread = (row48 == work_row).astype(jnp.bfloat16)
    slots = jnp.broadcast_to(slot_ref[...].astype(jnp.float32), (8, TOK)).astype(jnp.bfloat16)
    col_slot = jnp.dot(slots, spread, preferred_element_type=jnp.float32)[0:1].astype(jnp.int32)
    usable = jnp.where(col < 2 * WIN, 2, jnp.where(col < 3 * WIN, kept, 5 - kept)) >= jnp.where(
        col < 2 * WIN, 0, 3
    )
    col_slot = jnp.where(usable, col_slot, -1)

    half_scale = math.log2(math.e) / math.sqrt(HEAD)
    lane = lax.broadcasted_iota(jnp.int32, (1, 256), 1)
    head_mask = []
    ones_mask = []
    row128 = lax.broadcasted_iota(jnp.int32, (128, 256), 0)
    lane128 = lax.broadcasted_iota(jnp.int32, (128, 256), 1)
    for pair in range(4):
        low = 32 * pair
        first = ((lane >= low) & (lane < low + HEAD)).astype(jnp.bfloat16)
        second = ((lane >= low + HEAD) & (lane < low + 2 * HEAD)).astype(jnp.bfloat16)
        head_mask.append((first, second))
        start = jnp.where(row128 < WIN, low, low + HEAD)
        ones_mask.append(((lane128 >= start) & (lane128 < start + HEAD)).astype(jnp.bfloat16))
    left = lax.broadcasted_iota(jnp.int32, (WIN, 128), 1) < WIN

    def attend(slot, row):
        for group in range(2):
            num = [None] * 5
            den = [None] * 5
            for pair in range(4):
                at = HALF * group + 128 * pair
                q = qkv[slot, :, at : at + 256]
                k = qkv[slot, :, D + at : D + at + 256]
                v = qkv[slot, :, 2 * D + at : 2 * D + at + 256]
                first, second = head_mask[pair]
                keys = jnp.concatenate([k * first, k * second], axis=0)
                s = lax.dot_general(
                    q, keys, (((1,), (1,)), ((), ())), preferred_element_type=jnp.float32
                )
                top_a = jnp.max(jnp.where(left, s, -jnp.inf), axis=1, keepdims=True)
                top_b = jnp.max(jnp.where(left, -jnp.inf, s), axis=1, keepdims=True)
                p = jnp.exp2((s - jnp.where(left, top_a, top_b)) * half_scale).astype(jnp.bfloat16)
                values = jnp.concatenate([v * first, v * second], axis=0)
                o = jnp.dot(p, values, preferred_element_type=jnp.float32)
                total = jnp.dot(p, ones_mask[pair], preferred_element_type=jnp.float32)
                for part in range(2):
                    cut = slice(128 * part, 128 * part + 128)
                    tile = pair + part
                    num[tile] = o[:, cut] if num[tile] is None else num[tile] + o[:, cut]
                    den[tile] = total[:, cut] if den[tile] is None else den[tile] + total[:, cut]
            for tile in range(5):
                at = HALF * group + 128 * tile
                att[pl.ds(row, WIN), at : at + 128] = (num[tile] / den[tile]).astype(jnp.bfloat16)

    def project(rows, resid_rows):
        hidden = jnp.dot(att[0:rows], weight[...], preferred_element_type=jnp.float32)
        hidden = hidden + bias + resid_rows.astype(jnp.float32)
        inv_rms = lax.rsqrt(jnp.mean(hidden * hidden, axis=-1, keepdims=True) + 1e-06)
        return (hidden * inv_rms * gain).astype(jnp.bfloat16)

    loads[0].wait()
    attend(last_live, 0)
    loads[1].wait()
    loads[2].wait()
    lend[...] = project(WIN, resid[last_live])

    pl.semaphore_wait(barrier, len(PARTNERS) + 1)
    lending = pltpu.make_async_remote_copy(
        src_ref=lend,
        dst_ref=normed.at[pl.ds(3 * WIN, WIN)],
        send_sem=lend_sem.at[0],
        recv_sem=lend_sem.at[1],
        device_id=next_enc,
        device_id_type=MESH,
    )
    lending.start()

    for block in range(3):
        attend(block, WIN * block)
    normed[0 : 3 * WIN] = project(3 * WIN, resid[0:3].reshape(3 * WIN, D))

    r = lax.broadcasted_iota(jnp.int32, (TOK * 8, 4 * WIN), 0)
    c = lax.broadcasted_iota(jnp.int32, (TOK * 8, 4 * WIN), 1)
    target = (me + place_offset(r // 8)) & (SEQ - 1)
    hit = (target == col_slot) & ((r & 3) == (c & 3))
    pick_low = (hit & ((r & 4) == 0)).astype(jnp.bfloat16)
    pick_high = (hit & ((r & 4) != 0)).astype(jnp.bfloat16)

    lending.wait()
    placed = jnp.dot(pick_low, normed[:, :HALF], preferred_element_type=jnp.float32)
    placed = placed + jnp.dot(pick_high, normed[:, HALF:], preferred_element_type=jnp.float32)
    outgoing[...] = placed.astype(jnp.bfloat16).reshape(TOK, 8, HALF)

    own = pltpu.make_async_copy(outgoing.at[0], out_hbm.at[0], own_sem)
    own.start()

    jumps = {}
    arrived = set()
    lasts = []
    group_of = {t: i for i, g in enumerate(GROUPS) for t in range(g[2], g[3])}

    def held(first, count, done):
        if done == 0:
            return outgoing.at[pl.ds(first, count)]
        return relay.at[done - 1, pl.ds(first, count)]

    def need(group, done):
        if done and (group, done) not in arrived:
            arrived.add((group, done))
            jumps[group, done].wait_recv()

    for item in ORDER:
        if item[0] == "jump":
            _, group, turn = item
            sign, _, first, end = GROUPS[group]
            need(group, turn - 1)
            sem = group * ROUNDS + turn - 1
            copy = pltpu.make_async_remote_copy(
                src_ref=held(first, end - first, turn - 1),
                dst_ref=relay.at[turn - 1, pl.ds(first, end - first)],
                send_sem=jump_send.at[sem],
                recv_sem=jump_recv.at[sem],
                device_id=along_seq(sign * JUMP),
                device_id_type=MESH,
            )
            copy.start()
            jumps[group, turn] = copy
        else:
            token = item[1]
            done = full_jumps(OFFSETS[token])
            if done:
                need(group_of[token], done)
            copy = pltpu.make_async_remote_copy(
                src_ref=held(token, 1, done),
                dst_ref=out_hbm.at[pl.ds(token, 1)],
                send_sem=last_send.at[token],
                recv_sem=last_recv.at[token],
                device_id=along_seq(last_offset(OFFSETS[token])),
                device_id_type=MESH,
            )
            copy.start()
            lasts.append(copy)
    own.wait()
    for copy in jumps.values():
        copy.wait_send()
    for copy in lasts:
        copy.wait()


def place_kernel(row_ref, arrived_ref, out_ref):
    me = lax.axis_index("seq")
    rows = TOK * 8
    g = lax.broadcasted_iota(jnp.int32, (SEQ, rows), 0)
    c = lax.broadcasted_iota(jnp.int32, (SEQ, rows), 1)
    sender = (me - place_offset(c // 8)) & (SEQ - 1)
    lm = jnp.broadcast_to(row_ref[...].astype(jnp.float32), (8, SEQ)).astype(jnp.bfloat16)
    row_of = jnp.dot(lm, (g == sender).astype(jnp.bfloat16), preferred_element_type=jnp.float32)
    row_of = row_of[0:1].astype(jnp.int32)
    r = lax.broadcasted_iota(jnp.int32, (TOK, rows), 0)
    c = lax.broadcasted_iota(jnp.int32, (TOK, rows), 1)
    hit = r == row_of
    arrived = arrived_ref[...].reshape(rows, HALF)
    for part in range(8):
        half, patch = part // 4, part % 4
        pick = (hit & ((c & 7) == part)).astype(jnp.bfloat16)
        cut = jnp.dot(pick, arrived, preferred_element_type=jnp.float32)
        at = patch * D + half * HALF
        out_ref[:, at : at + HALF] = cut.astype(jnp.bfloat16)


def per_device(
    qkv, resid, block_count, send_count, send_slot, lm_row, out_weight, out_bias, norm_gain
):
    vmem = pl.BlockSpec(memory_space=pltpu.VMEM)
    smem = pl.BlockSpec(memory_space=pltpu.SMEM)
    hbm = pl.BlockSpec(memory_space=pl.ANY)
    dma = pltpu.SemaphoreType.DMA
    arrived = pl.pallas_call(
        encode_kernel,
        out_shape=jax.ShapeDtypeStruct((TOK, 8, HALF), jnp.bfloat16),
        in_specs=[hbm, hbm, smem, smem, vmem, hbm, vmem, vmem],
        out_specs=hbm,
        scratch_shapes=[
            pltpu.VMEM(qkv.shape, jnp.bfloat16),
            pltpu.VMEM(resid.shape, jnp.bfloat16),
            pltpu.VMEM((D, D), jnp.bfloat16),
            pltpu.VMEM((3 * WIN, D), jnp.bfloat16),
            pltpu.VMEM((WIN, D), jnp.bfloat16),
            pltpu.VMEM((4 * WIN, D), jnp.bfloat16),
            pltpu.VMEM((TOK, 8, HALF), jnp.bfloat16),
            pltpu.VMEM((ROUNDS, TOK, 8, HALF), jnp.bfloat16),
            dma((3,)),
            dma((2,)),
            dma((len(GROUPS) * ROUNDS,)),
            dma((len(GROUPS) * ROUNDS,)),
            dma((TOK,)),
            dma((TOK,)),
            dma,
        ],
        compiler_params=pltpu.CompilerParams(collective_id=0, has_side_effects=True),
    )(
        qkv,
        resid,
        block_count,
        send_count,
        send_slot,
        out_weight,
        out_bias.reshape(1, D),
        norm_gain.reshape(1, D),
    )
    placed = pl.pallas_call(
        place_kernel,
        out_shape=jax.ShapeDtypeStruct((TOK, 4 * D), jnp.bfloat16),
        in_specs=[vmem, vmem],
        out_specs=vmem,
    )(lm_row, arrived)
    return placed[None]


def solution(mesh):
    placed = (
        P("enc", "seq", None),
        P("enc", "seq", None),
        P("enc", "seq"),
        P("enc", "seq"),
        P("enc", "seq"),
        P("enc", "seq"),
        P(),
        P(),
        P(),
    )
    return jax.shard_map(
        per_device, mesh=mesh, in_specs=placed, out_specs=P("enc", "seq", None), check_vma=False
    )
```

```python
import functools
import math

import jax
import jax.numpy as jnp
from jax import lax
from jax.experimental import pallas as pl
from jax.experimental.pallas import tpu as pltpu
from jax.sharding import PartitionSpec as P

MESH = pl.DeviceIdType.MESH
D = 1280
HALF = 640
HEAD = 80
WIN = 64
SEQ = 64
ENC = 16
TOK = 48
RELAY = 16
NEAR = [d for d in range(-RELAY, RELAY + 1) if d]


def place_offset(place):
    return jnp.where(place < 24, place, jnp.where(place < 27, place + 8, 82 - place))


def encode_kernel(
    qkv_hbm,
    resid_hbm,
    count_ref,
    lent_ref,
    slot_ref,
    weight_hbm,
    bias_ref,
    gain_ref,
    out_hbm,
    qkv,
    resid,
    weight,
    att,
    lend,
    normed,
    outgoing,
    relay,
    load_sem,
    lend_sem,
    relay_send,
    relay_recv,
    token_send,
    token_recv,
    own_sem,
    far_sem,
):
    me = lax.axis_index("seq")
    enc = lax.axis_index("enc")

    def along_seq(offset):
        return (enc, lax.rem(me + offset + 2 * SEQ, SEQ))

    next_enc = (lax.rem(enc + 1, ENC), me)
    prev_enc = (lax.rem(enc + ENC - 1, ENC), me)

    barrier = pltpu.get_barrier_semaphore()
    for offset in NEAR:
        pl.semaphore_signal(barrier, inc=1, device_id=along_seq(offset), device_id_type=MESH)
    pl.semaphore_signal(barrier, inc=1, device_id=prev_enc, device_id_type=MESH)

    loads = [
        pltpu.make_async_copy(qkv_hbm, qkv, load_sem.at[0]),
        pltpu.make_async_copy(weight_hbm, weight, load_sem.at[1]),
        pltpu.make_async_copy(resid_hbm, resid, load_sem.at[2]),
    ]
    for copy in loads:
        copy.start()

    live = count_ref[0, 0]
    kept = live - lent_ref[0, 0]
    last_live = jnp.clip(live - 1, 0, 3)
    bias = bias_ref[...].astype(jnp.float32).reshape(1, D)
    gain = gain_ref[...].astype(jnp.float32).reshape(1, D)

    col = lax.broadcasted_iota(jnp.int32, (1, 4 * WIN), 1)
    row48 = lax.broadcasted_iota(jnp.int32, (TOK, 4 * WIN), 0)
    col48 = lax.broadcasted_iota(jnp.int32, (TOK, 4 * WIN), 1)
    work_row = jnp.where(col48 < 3 * WIN, col48 // 4, (col48 - WIN) // 4)
    spread = (row48 == work_row).astype(jnp.bfloat16)
    slots = jnp.broadcast_to(slot_ref[...].astype(jnp.float32), (8, TOK)).astype(jnp.bfloat16)
    col_slot = jnp.dot(slots, spread, preferred_element_type=jnp.float32)[0:1].astype(jnp.int32)
    usable = jnp.where(col < 2 * WIN, 2, jnp.where(col < 3 * WIN, kept, 5 - kept)) >= jnp.where(
        col < 2 * WIN, 0, 3
    )
    col_slot = jnp.where(usable, col_slot, -1)

    half_scale = math.log2(math.e) / math.sqrt(HEAD)
    lane = lax.broadcasted_iota(jnp.int32, (1, 256), 1)
    head_mask = []
    ones_mask = []
    row128 = lax.broadcasted_iota(jnp.int32, (128, 256), 0)
    lane128 = lax.broadcasted_iota(jnp.int32, (128, 256), 1)
    for pair in range(4):
        low = 32 * pair
        first = ((lane >= low) & (lane < low + HEAD)).astype(jnp.bfloat16)
        second = ((lane >= low + HEAD) & (lane < low + 2 * HEAD)).astype(jnp.bfloat16)
        head_mask.append((first, second))
        start = jnp.where(row128 < WIN, low, low + HEAD)
        ones_mask.append(((lane128 >= start) & (lane128 < start + HEAD)).astype(jnp.bfloat16))
    left = lax.broadcasted_iota(jnp.int32, (WIN, 128), 1) < WIN

    def attend(slot, row):
        for group in range(2):
            num = [None] * 5
            den = [None] * 5
            for pair in range(4):
                at = HALF * group + 128 * pair
                q = qkv[slot, :, at : at + 256]
                k = qkv[slot, :, D + at : D + at + 256]
                v = qkv[slot, :, 2 * D + at : 2 * D + at + 256]
                first, second = head_mask[pair]
                keys = jnp.concatenate([k * first, k * second], axis=0)
                s = lax.dot_general(
                    q, keys, (((1,), (1,)), ((), ())), preferred_element_type=jnp.float32
                )
                top_a = jnp.max(jnp.where(left, s, -jnp.inf), axis=1, keepdims=True)
                top_b = jnp.max(jnp.where(left, -jnp.inf, s), axis=1, keepdims=True)
                p = jnp.exp2((s - jnp.where(left, top_a, top_b)) * half_scale).astype(jnp.bfloat16)
                values = jnp.concatenate([v * first, v * second], axis=0)
                o = jnp.dot(p, values, preferred_element_type=jnp.float32)
                total = jnp.dot(p, ones_mask[pair], preferred_element_type=jnp.float32)
                for part in range(2):
                    cut = slice(128 * part, 128 * part + 128)
                    tile = pair + part
                    num[tile] = o[:, cut] if num[tile] is None else num[tile] + o[:, cut]
                    den[tile] = total[:, cut] if den[tile] is None else den[tile] + total[:, cut]
            for tile in range(5):
                at = HALF * group + 128 * tile
                att[pl.ds(row, WIN), at : at + 128] = (num[tile] / den[tile]).astype(jnp.bfloat16)

    def project(rows, resid_rows):
        hidden = jnp.dot(att[0:rows], weight[...], preferred_element_type=jnp.float32)
        hidden = hidden + bias + resid_rows.astype(jnp.float32)
        inv_rms = lax.rsqrt(jnp.mean(hidden * hidden, axis=-1, keepdims=True) + 1e-06)
        return (hidden * inv_rms * gain).astype(jnp.bfloat16)

    loads[0].wait()
    attend(last_live, 0)
    loads[1].wait()
    loads[2].wait()
    lend[...] = project(WIN, resid[last_live])

    attend(0, 0)
    pl.semaphore_wait(barrier, len(NEAR) + 1)
    lending = pltpu.make_async_remote_copy(
        src_ref=lend,
        dst_ref=normed.at[pl.ds(3 * WIN, WIN)],
        send_sem=lend_sem.at[0],
        recv_sem=lend_sem.at[1],
        device_id=next_enc,
        device_id_type=MESH,
    )
    lending.start()
    for offset in (RELAY, -RELAY):
        pl.semaphore_signal(far_sem, inc=1, device_id=along_seq(offset), device_id_type=MESH)

    attend(1, WIN)
    attend(2, 2 * WIN)
    normed[0 : 3 * WIN] = project(3 * WIN, resid[0:3].reshape(3 * WIN, D))

    r = lax.broadcasted_iota(jnp.int32, (TOK * 8, 4 * WIN), 0)
    c = lax.broadcasted_iota(jnp.int32, (TOK * 8, 4 * WIN), 1)
    target = (me + place_offset(r // 8)) & (SEQ - 1)
    hit = (target == col_slot) & ((r & 3) == (c & 3))
    pick_low = (hit & ((r & 4) == 0)).astype(jnp.bfloat16)
    pick_high = (hit & ((r & 4) != 0)).astype(jnp.bfloat16)

    lending.wait()
    placed = jnp.dot(pick_low, normed[:, :HALF], preferred_element_type=jnp.float32)
    placed = placed + jnp.dot(pick_high, normed[:, HALF:], preferred_element_type=jnp.float32)
    outgoing[...] = placed.astype(jnp.bfloat16).reshape(TOK, 8, HALF)

    own = pltpu.make_async_copy(outgoing.at[0], out_hbm.at[0], own_sem)
    own.start()

    pl.semaphore_wait(far_sem, 2)

    def token(place, device):
        return pltpu.make_async_remote_copy(
            src_ref=outgoing.at[pl.ds(place, 1)],
            dst_ref=out_hbm.at[pl.ds(place, 1)],
            send_sem=token_send.at[place],
            recv_sem=token_recv.at[place],
            device_id=device,
            device_id_type=MESH,
        )

    first_leg = pltpu.make_async_remote_copy(
        src_ref=outgoing.at[pl.ds(25, 2)],
        dst_ref=relay,
        send_sem=relay_send,
        recv_sem=relay_recv,
        device_id=along_seq(RELAY),
        device_id_type=MESH,
    )
    first_leg.start()
    token(24, along_seq(32)).start()

    wrapping = jnp.clip(me - 40, 0, 23)
    low = jnp.clip(me - 8, 0, 21)

    def up(i):
        return jnp.where(i < wrapping, SEQ - me + i, jnp.minimum(SEQ - 1 - me, 23) - (i - wrapping))

    def down(i):
        return jnp.where(i < low, 8 + low - i, 29 - (i - low))

    def send_up(i):
        offset = up(i)
        token(offset, along_seq(offset)).start()

    @pl.loop(0, 21)
    def _(i):
        send_up(i)
        offset = down(i)
        token(18 + offset, along_seq(-offset)).start()

    send_up(21)
    send_up(22)
    first_leg.wait_recv()
    for q in range(2):
        pltpu.make_async_remote_copy(
            src_ref=relay.at[pl.ds(q, 1)],
            dst_ref=out_hbm.at[pl.ds(25 + q, 1)],
            send_sem=token_send.at[25 + q],
            recv_sem=token_recv.at[25 + q],
            device_id=along_seq(RELAY + 1 + q),
            device_id_type=MESH,
        ).start()
    own.wait()
    first_leg.wait_send()

    @pl.loop(1, TOK)
    def _(place):
        token(place, along_seq(1)).wait()


def place_kernel(row_ref, arrived_ref, out_ref):
    me = lax.axis_index("seq")
    rows = TOK * 8
    g = lax.broadcasted_iota(jnp.int32, (SEQ, rows), 0)
    c = lax.broadcasted_iota(jnp.int32, (SEQ, rows), 1)
    sender = (me - place_offset(c // 8)) & (SEQ - 1)
    lm = jnp.broadcast_to(row_ref[...].astype(jnp.float32), (8, SEQ)).astype(jnp.bfloat16)
    row_of = jnp.dot(lm, (g == sender).astype(jnp.bfloat16), preferred_element_type=jnp.float32)
    row_of = row_of[0:1].astype(jnp.int32)
    r = lax.broadcasted_iota(jnp.int32, (TOK, rows), 0)
    c = lax.broadcasted_iota(jnp.int32, (TOK, rows), 1)
    hit = r == row_of
    arrived = arrived_ref[...].reshape(rows, HALF)
    for part in range(8):
        half, patch = part // 4, part % 4
        pick = (hit & ((c & 7) == part)).astype(jnp.bfloat16)
        cut = jnp.dot(pick, arrived, preferred_element_type=jnp.float32)
        at = patch * D + half * HALF
        out_ref[:, at : at + HALF] = cut.astype(jnp.bfloat16)


def per_device(
    qkv, resid, block_count, send_count, send_slot, lm_row, out_weight, out_bias, norm_gain
):
    vmem = pl.BlockSpec(memory_space=pltpu.VMEM)
    smem = pl.BlockSpec(memory_space=pltpu.SMEM)
    hbm = pl.BlockSpec(memory_space=pl.ANY)
    dma = pltpu.SemaphoreType.DMA
    arrived = pl.pallas_call(
        encode_kernel,
        out_shape=jax.ShapeDtypeStruct((TOK, 8, HALF), jnp.bfloat16),
        in_specs=[hbm, hbm, smem, smem, vmem, hbm, vmem, vmem],
        out_specs=hbm,
        scratch_shapes=[
            pltpu.VMEM(qkv.shape, jnp.bfloat16),
            pltpu.VMEM(resid.shape, jnp.bfloat16),
            pltpu.VMEM((D, D), jnp.bfloat16),
            pltpu.VMEM((3 * WIN, D), jnp.bfloat16),
            pltpu.VMEM((WIN, D), jnp.bfloat16),
            pltpu.VMEM((4 * WIN, D), jnp.bfloat16),
            pltpu.VMEM((TOK, 8, HALF), jnp.bfloat16),
            pltpu.VMEM((2, 8, HALF), jnp.bfloat16),
            dma((3,)),
            dma((2,)),
            dma,
            dma,
            dma((TOK,)),
            dma((TOK,)),
            dma,
            pltpu.SemaphoreType.REGULAR,
        ],
        compiler_params=pltpu.CompilerParams(collective_id=0, has_side_effects=True),
    )(
        qkv,
        resid,
        block_count,
        send_count,
        send_slot,
        out_weight,
        out_bias,
        norm_gain,
    )
    placed = pl.pallas_call(
        place_kernel,
        out_shape=jax.ShapeDtypeStruct((TOK, 4 * D), jnp.bfloat16),
        in_specs=[vmem, vmem],
        out_specs=vmem,
    )(lm_row, arrived)
    return placed[None]


def solution(mesh):
    placed = (
        P("enc", "seq", None),
        P("enc", "seq", None),
        P("enc", "seq"),
        P("enc", "seq"),
        P("enc", "seq"),
        P("enc", "seq"),
        P(),
        P(),
        P(),
    )
    return jax.shard_map(
        per_device, mesh=mesh, in_specs=placed, out_specs=P("enc", "seq", None), check_vma=False
    )
```

```python
import functools
import math

import jax
import jax.numpy as jnp
from jax import lax
from jax.experimental import pallas as pl
from jax.experimental.pallas import tpu as pltpu
from jax.sharding import PartitionSpec as P

MESH = pl.DeviceIdType.MESH
D = 1280
HALF = 640
HEAD = 80
WIN = 64
SEQ = 64
ENC = 16
TOK = 48
RELAY = 16
STEP = 8
NEAR = [d for d in range(-STEP, STEP + 1) if d]

RELAYED = ((25, 2), (47, 1))


def place_offset(place):
    return jnp.where(place < 24, place, jnp.where(place < 27, place + 8, 82 - place))


def encode_kernel(
    qkv_hbm,
    resid_hbm,
    count_ref,
    lent_ref,
    slot_ref,
    weight_hbm,
    bias_ref,
    gain_ref,
    out_hbm,
    qkv,
    resid,
    weight,
    att,
    lend,
    normed,
    outgoing,
    relay,
    load_sem,
    lend_sem,
    relay_send,
    relay_recv,
    token_send,
    token_recv,
    own_sem,
    step_sem,
    far_sem,
):
    me = lax.axis_index("seq")
    enc = lax.axis_index("enc")

    def along_seq(offset):
        return (enc, lax.rem(me + offset + 2 * SEQ, SEQ))

    next_enc = (lax.rem(enc + 1, ENC), me)
    prev_enc = (lax.rem(enc + ENC - 1, ENC), me)

    barrier = pltpu.get_barrier_semaphore()
    for offset in NEAR:
        pl.semaphore_signal(barrier, inc=1, device_id=along_seq(offset), device_id_type=MESH)
    pl.semaphore_signal(barrier, inc=1, device_id=prev_enc, device_id_type=MESH)

    loads = [
        pltpu.make_async_copy(qkv_hbm, qkv, load_sem.at[0]),
        pltpu.make_async_copy(weight_hbm, weight, load_sem.at[1]),
        pltpu.make_async_copy(resid_hbm, resid, load_sem.at[2]),
    ]
    for copy in loads:
        copy.start()

    live = count_ref[0, 0]
    kept = live - lent_ref[0, 0]
    last_live = jnp.clip(live - 1, 0, 3)
    bias = bias_ref[...].astype(jnp.float32).reshape(1, D)
    gain = gain_ref[...].astype(jnp.float32).reshape(1, D)

    col = lax.broadcasted_iota(jnp.int32, (1, 4 * WIN), 1)
    row48 = lax.broadcasted_iota(jnp.int32, (TOK, 4 * WIN), 0)
    col48 = lax.broadcasted_iota(jnp.int32, (TOK, 4 * WIN), 1)
    work_row = jnp.where(col48 < 3 * WIN, col48 // 4, (col48 - WIN) // 4)
    spread = (row48 == work_row).astype(jnp.bfloat16)
    slots = jnp.broadcast_to(slot_ref[...].astype(jnp.float32), (8, TOK)).astype(jnp.bfloat16)
    col_slot = jnp.dot(slots, spread, preferred_element_type=jnp.float32)[0:1].astype(jnp.int32)
    usable = jnp.where(col < 2 * WIN, 2, jnp.where(col < 3 * WIN, kept, 5 - kept)) >= jnp.where(
        col < 2 * WIN, 0, 3
    )
    col_slot = jnp.where(usable, col_slot, -1)

    half_scale = math.log2(math.e) / math.sqrt(HEAD)
    lane = lax.broadcasted_iota(jnp.int32, (1, 256), 1)
    head_mask = []
    ones_mask = []
    row128 = lax.broadcasted_iota(jnp.int32, (128, 256), 0)
    lane128 = lax.broadcasted_iota(jnp.int32, (128, 256), 1)
    for pair in range(4):
        low = 32 * pair
        first = ((lane >= low) & (lane < low + HEAD)).astype(jnp.bfloat16)
        second = ((lane >= low + HEAD) & (lane < low + 2 * HEAD)).astype(jnp.bfloat16)
        head_mask.append((first, second))
        start = jnp.where(row128 < WIN, low, low + HEAD)
        ones_mask.append(((lane128 >= start) & (lane128 < start + HEAD)).astype(jnp.bfloat16))
    left = lax.broadcasted_iota(jnp.int32, (WIN, 128), 1) < WIN

    def attend(slot, row):
        for group in range(2):
            num = [None] * 5
            den = [None] * 5
            for pair in range(4):
                at = HALF * group + 128 * pair
                q = qkv[slot, :, at : at + 256]
                k = qkv[slot, :, D + at : D + at + 256]
                v = qkv[slot, :, 2 * D + at : 2 * D + at + 256]
                first, second = head_mask[pair]
                keys = jnp.concatenate([k * first, k * second], axis=0)
                s = lax.dot_general(
                    q, keys, (((1,), (1,)), ((), ())), preferred_element_type=jnp.float32
                )
                top_a = jnp.max(jnp.where(left, s, -jnp.inf), axis=1, keepdims=True)
                top_b = jnp.max(jnp.where(left, -jnp.inf, s), axis=1, keepdims=True)
                p = jnp.exp2((s - jnp.where(left, top_a, top_b)) * half_scale).astype(jnp.bfloat16)
                values = jnp.concatenate([v * first, v * second], axis=0)
                o = jnp.dot(p, values, preferred_element_type=jnp.float32)
                total = jnp.dot(p, ones_mask[pair], preferred_element_type=jnp.float32)
                for part in range(2):
                    cut = slice(128 * part, 128 * part + 128)
                    tile = pair + part
                    num[tile] = o[:, cut] if num[tile] is None else num[tile] + o[:, cut]
                    den[tile] = total[:, cut] if den[tile] is None else den[tile] + total[:, cut]
            for tile in range(5):
                at = HALF * group + 128 * tile
                att[pl.ds(row, WIN), at : at + 128] = (num[tile] / den[tile]).astype(jnp.bfloat16)

    def project(rows, resid_rows):
        hidden = jnp.dot(att[0:rows], weight[...], preferred_element_type=jnp.float32)
        hidden = hidden + bias + resid_rows.astype(jnp.float32)
        inv_rms = lax.rsqrt(jnp.mean(hidden * hidden, axis=-1, keepdims=True) + 1e-06)
        return (hidden * inv_rms * gain).astype(jnp.bfloat16)

    loads[0].wait()
    attend(last_live, 0)
    pl.semaphore_wait(barrier, len(NEAR) + 1)
    for offset in (STEP, -STEP):
        pl.semaphore_signal(step_sem, inc=1, device_id=along_seq(offset), device_id_type=MESH)
    loads[1].wait()
    loads[2].wait()
    lend[...] = project(WIN, resid[last_live])

    lending = pltpu.make_async_remote_copy(
        src_ref=lend,
        dst_ref=normed.at[pl.ds(3 * WIN, WIN)],
        send_sem=lend_sem.at[0],
        recv_sem=lend_sem.at[1],
        device_id=next_enc,
        device_id_type=MESH,
    )
    lending.start()

    attend(0, 0)
    pl.semaphore_wait(step_sem, 2)
    for offset in (RELAY, -RELAY):
        pl.semaphore_signal(far_sem, inc=1, device_id=along_seq(offset), device_id_type=MESH)

    attend(1, WIN)
    attend(2, 2 * WIN)
    normed[0 : 3 * WIN] = project(3 * WIN, resid[0:3].reshape(3 * WIN, D))

    r = lax.broadcasted_iota(jnp.int32, (TOK * 8, 4 * WIN), 0)
    c = lax.broadcasted_iota(jnp.int32, (TOK * 8, 4 * WIN), 1)
    target = (me + place_offset(r // 8)) & (SEQ - 1)
    hit = (target == col_slot) & ((r & 3) == (c & 3))
    pick_low = (hit & ((r & 4) == 0)).astype(jnp.bfloat16)
    pick_high = (hit & ((r & 4) != 0)).astype(jnp.bfloat16)

    def picked(rows):
        low_half = jnp.dot(
            pick_low[:, rows], normed[rows, :HALF], preferred_element_type=jnp.float32
        )
        return low_half + jnp.dot(
            pick_high[:, rows], normed[rows, HALF:], preferred_element_type=jnp.float32
        )

    placed = picked(slice(0, 2 * WIN))
    lending.wait()
    placed = placed + picked(slice(2 * WIN, 4 * WIN))
    outgoing[...] = placed.astype(jnp.bfloat16).reshape(TOK, 8, HALF)

    own = pltpu.make_async_copy(outgoing.at[0], out_hbm.at[0], own_sem)
    own.start()

    pl.semaphore_wait(far_sem, 2)

    def token(place, device):
        return pltpu.make_async_remote_copy(
            src_ref=outgoing.at[pl.ds(place, 1)],
            dst_ref=out_hbm.at[pl.ds(place, 1)],
            send_sem=token_send.at[place],
            recv_sem=token_recv.at[place],
            device_id=device,
            device_id_type=MESH,
        )

    first_legs = []
    for leg, (place, count) in enumerate(RELAYED):
        first_legs.append(
            pltpu.make_async_remote_copy(
                src_ref=outgoing.at[pl.ds(place, count)],
                dst_ref=relay.at[pl.ds(2 * leg, count)],
                send_sem=relay_send.at[leg],
                recv_sem=relay_recv.at[leg],
                device_id=along_seq(RELAY),
                device_id_type=MESH,
            )
        )
        first_legs[-1].start()
    token(24, along_seq(32)).start()

    wrapping = jnp.clip(me - 40, 0, 23)
    low = jnp.clip(me - 8, 0, 20)

    def up(i):
        return jnp.where(i < wrapping, SEQ - me + i, jnp.minimum(SEQ - 1 - me, 23) - (i - wrapping))

    def down(i):
        return jnp.where(i < low, 8 + low - i, 28 - (i - low))

    @pl.loop(0, 20)
    def _(i):
        offset = down(i)
        token(18 + offset, along_seq(-offset)).start()

    for leg, (place, count) in enumerate(RELAYED):
        first_legs[leg].wait_recv()
        for q in range(count):
            held = 2 * leg + q
            pltpu.make_async_remote_copy(
                src_ref=relay.at[pl.ds(held, 1)],
                dst_ref=out_hbm.at[pl.ds(place + q, 1)],
                send_sem=token_send.at[place + q],
                recv_sem=token_recv.at[place + q],
                device_id=along_seq(33 + held - RELAY),
                device_id_type=MESH,
            ).start()

    @pl.loop(0, 23)
    def _(i):
        offset = up(i)
        token(offset, along_seq(offset)).start()

    own.wait()
    for leg in first_legs:
        leg.wait_send()

    @pl.loop(1, TOK)
    def _(place):
        token(place, along_seq(1)).wait()


def place_kernel(row_ref, arrived_ref, out_ref):
    me = lax.axis_index("seq")
    rows = TOK * 8
    g = lax.broadcasted_iota(jnp.int32, (SEQ, rows), 0)
    c = lax.broadcasted_iota(jnp.int32, (SEQ, rows), 1)
    sender = (me - place_offset(c // 8)) & (SEQ - 1)
    lm = jnp.broadcast_to(row_ref[...].astype(jnp.float32), (8, SEQ)).astype(jnp.bfloat16)
    row_of = jnp.dot(lm, (g == sender).astype(jnp.bfloat16), preferred_element_type=jnp.float32)
    row_of = row_of[0:1].astype(jnp.int32)
    r = lax.broadcasted_iota(jnp.int32, (TOK, rows), 0)
    c = lax.broadcasted_iota(jnp.int32, (TOK, rows), 1)
    hit = r == row_of
    arrived = arrived_ref[...].reshape(rows, HALF)
    pick = jnp.concatenate(
        [(hit & ((c & 7) == part)).astype(jnp.bfloat16) for part in range(8)], axis=0
    )
    cut = jnp.dot(pick, arrived, preferred_element_type=jnp.float32).astype(jnp.bfloat16)
    for part in range(8):
        at = part % 4 * D + part // 4 * HALF
        out_ref[:, at : at + HALF] = cut[TOK * part : TOK * (part + 1)]


def per_device(
    qkv, resid, block_count, send_count, send_slot, lm_row, out_weight, out_bias, norm_gain
):
    vmem = pl.BlockSpec(memory_space=pltpu.VMEM)
    smem = pl.BlockSpec(memory_space=pltpu.SMEM)
    hbm = pl.BlockSpec(memory_space=pl.ANY)
    dma = pltpu.SemaphoreType.DMA
    arrived = pl.pallas_call(
        encode_kernel,
        out_shape=jax.ShapeDtypeStruct((TOK, 8, HALF), jnp.bfloat16),
        in_specs=[hbm, hbm, smem, smem, vmem, hbm, vmem, vmem],
        out_specs=hbm,
        scratch_shapes=[
            pltpu.VMEM(qkv.shape, jnp.bfloat16),
            pltpu.VMEM(resid.shape, jnp.bfloat16),
            pltpu.VMEM((D, D), jnp.bfloat16),
            pltpu.VMEM((3 * WIN, D), jnp.bfloat16),
            pltpu.VMEM((WIN, D), jnp.bfloat16),
            pltpu.VMEM((4 * WIN, D), jnp.bfloat16),
            pltpu.VMEM((TOK, 8, HALF), jnp.bfloat16),
            pltpu.VMEM((3, 8, HALF), jnp.bfloat16),
            dma((3,)),
            dma((2,)),
            dma((2,)),
            dma((2,)),
            dma((TOK,)),
            dma((TOK,)),
            dma,
            pltpu.SemaphoreType.REGULAR,
            pltpu.SemaphoreType.REGULAR,
        ],
        compiler_params=pltpu.CompilerParams(collective_id=0, has_side_effects=True),
    )(
        qkv,
        resid,
        block_count,
        send_count,
        send_slot,
        out_weight,
        out_bias,
        norm_gain,
    )
    placed = pl.pallas_call(
        place_kernel,
        out_shape=jax.ShapeDtypeStruct((TOK, 4 * D), jnp.bfloat16),
        in_specs=[vmem, vmem],
        out_specs=vmem,
    )(lm_row, arrived)
    return placed[None]


def solution(mesh):
    placed = (
        P("enc", "seq", None),
        P("enc", "seq", None),
        P("enc", "seq"),
        P("enc", "seq"),
        P("enc", "seq"),
        P("enc", "seq"),
        P(),
        P(),
        P(),
    )
    return jax.shard_map(
        per_device, mesh=mesh, in_specs=placed, out_specs=P("enc", "seq", None), check_vma=False
    )
```

```python
import functools
import math

import jax
import jax.numpy as jnp
from jax import lax
from jax.experimental import pallas as pl
from jax.experimental.pallas import tpu as pltpu
from jax.sharding import PartitionSpec as P

MESH = pl.DeviceIdType.MESH
D = 1280
HALF = 640
HEAD = 80
WIN = 64
SEQ = 64
ENC = 16
TOK = 48
RELAY = 16
STEP = 8
NEAR = [d for d in range(-STEP, STEP + 1) if d]

RELAYED = ((25, 2), (47, 1))


def place_offset(place):
    return jnp.where(place < 24, place, jnp.where(place < 27, place + 8, 82 - place))


def encode_kernel(
    qkv_hbm,
    resid_hbm,
    count_ref,
    lent_ref,
    slot_ref,
    weight_hbm,
    bias_ref,
    gain_ref,
    out_hbm,
    first_qkv,
    qkv,
    resid,
    weight,
    att,
    lend,
    normed,
    outgoing,
    relay,
    load_sem,
    lend_sem,
    relay_send,
    relay_recv,
    token_send,
    token_recv,
    own_sem,
    step_sem,
    far_sem,
):
    me = lax.axis_index("seq")
    enc = lax.axis_index("enc")

    def along_seq(offset):
        return (enc, lax.rem(me + offset + 2 * SEQ, SEQ))

    next_enc = (lax.rem(enc + 1, ENC), me)
    prev_enc = (lax.rem(enc + ENC - 1, ENC), me)

    barrier = pltpu.get_barrier_semaphore()
    for offset in NEAR:
        pl.semaphore_signal(barrier, inc=1, device_id=along_seq(offset), device_id_type=MESH)
    pl.semaphore_signal(barrier, inc=1, device_id=prev_enc, device_id_type=MESH)

    later = pl.ds(1, 3)
    loads = [
        pltpu.make_async_copy(qkv_hbm.at[later], qkv, load_sem.at[0]),
        pltpu.make_async_copy(weight_hbm, weight, load_sem.at[1]),
        pltpu.make_async_copy(resid_hbm, resid, load_sem.at[2]),
        pltpu.make_async_copy(qkv_hbm.at[pl.ds(0, 1)], first_qkv, load_sem.at[3]),
    ]
    for copy in loads:
        copy.start()

    live = count_ref[0, 0]
    kept = live - lent_ref[0, 0]
    last_live = jnp.clip(live - 1, 1, 3)
    bias = bias_ref[...].astype(jnp.float32).reshape(1, D)
    gain = gain_ref[...].astype(jnp.float32).reshape(1, D)

    col = lax.broadcasted_iota(jnp.int32, (1, 4 * WIN), 1)
    row48 = lax.broadcasted_iota(jnp.int32, (TOK, 4 * WIN), 0)
    col48 = lax.broadcasted_iota(jnp.int32, (TOK, 4 * WIN), 1)
    work_row = jnp.where(col48 < 3 * WIN, col48 // 4, (col48 - WIN) // 4)
    spread = (row48 == work_row).astype(jnp.bfloat16)
    slots = jnp.broadcast_to(slot_ref[...].astype(jnp.float32), (8, TOK)).astype(jnp.bfloat16)
    col_slot = jnp.dot(slots, spread, preferred_element_type=jnp.float32)[0:1].astype(jnp.int32)
    usable = jnp.where(col < 2 * WIN, 2, jnp.where(col < 3 * WIN, kept, 5 - kept)) >= jnp.where(
        col < 2 * WIN, 0, 3
    )
    col_slot = jnp.where(usable, col_slot, -1)

    half_scale = math.log2(math.e) / math.sqrt(HEAD)
    lane = lax.broadcasted_iota(jnp.int32, (1, 256), 1)
    head_mask = []
    ones_mask = []
    row128 = lax.broadcasted_iota(jnp.int32, (128, 256), 0)
    lane128 = lax.broadcasted_iota(jnp.int32, (128, 256), 1)
    for pair in range(4):
        low = 32 * pair
        first = ((lane >= low) & (lane < low + HEAD)).astype(jnp.bfloat16)
        second = ((lane >= low + HEAD) & (lane < low + 2 * HEAD)).astype(jnp.bfloat16)
        head_mask.append((first, second))
        start = jnp.where(row128 < WIN, low, low + HEAD)
        ones_mask.append(((lane128 >= start) & (lane128 < start + HEAD)).astype(jnp.bfloat16))
    left = lax.broadcasted_iota(jnp.int32, (WIN, 128), 1) < WIN

    def attend(qkv, slot, row):
        for group in range(2):
            num = [None] * 5
            den = [None] * 5
            for pair in range(4):
                at = HALF * group + 128 * pair
                q = qkv[slot, :, at : at + 256]
                k = qkv[slot, :, D + at : D + at + 256]
                v = qkv[slot, :, 2 * D + at : 2 * D + at + 256]
                first, second = head_mask[pair]
                keys = jnp.concatenate([k * first, k * second], axis=0)
                s = lax.dot_general(
                    q, keys, (((1,), (1,)), ((), ())), preferred_element_type=jnp.float32
                )
                top_a = jnp.max(jnp.where(left, s, -jnp.inf), axis=1, keepdims=True)
                top_b = jnp.max(jnp.where(left, -jnp.inf, s), axis=1, keepdims=True)
                p = jnp.exp2((s - jnp.where(left, top_a, top_b)) * half_scale).astype(jnp.bfloat16)
                values = jnp.concatenate([v * first, v * second], axis=0)
                o = jnp.dot(p, values, preferred_element_type=jnp.float32)
                total = jnp.dot(p, ones_mask[pair], preferred_element_type=jnp.float32)
                for part in range(2):
                    cut = slice(128 * part, 128 * part + 128)
                    tile = pair + part
                    num[tile] = o[:, cut] if num[tile] is None else num[tile] + o[:, cut]
                    den[tile] = total[:, cut] if den[tile] is None else den[tile] + total[:, cut]
            for tile in range(5):
                at = HALF * group + 128 * tile
                att[pl.ds(row, WIN), at : at + 128] = (num[tile] / den[tile]).astype(jnp.bfloat16)

    def project(rows, resid_rows):
        hidden = jnp.dot(att[0:rows], weight[...], preferred_element_type=jnp.float32)
        hidden = hidden + bias + resid_rows.astype(jnp.float32)
        inv_rms = lax.rsqrt(jnp.mean(hidden * hidden, axis=-1, keepdims=True) + 1e-06)
        return (hidden * inv_rms * gain).astype(jnp.bfloat16)

    loads[0].wait()
    attend(qkv, last_live - 1, 0)
    pl.semaphore_wait(barrier, len(NEAR) + 1)
    for offset in (STEP, -STEP):
        pl.semaphore_signal(step_sem, inc=1, device_id=along_seq(offset), device_id_type=MESH)
    loads[1].wait()
    loads[2].wait()
    lend[...] = project(WIN, resid[last_live])

    lending = pltpu.make_async_remote_copy(
        src_ref=lend,
        dst_ref=normed.at[pl.ds(3 * WIN, WIN)],
        send_sem=lend_sem.at[0],
        recv_sem=lend_sem.at[1],
        device_id=next_enc,
        device_id_type=MESH,
    )
    lending.start()

    loads[3].wait()
    attend(first_qkv, 0, 0)
    pl.semaphore_wait(step_sem, 2)
    for offset in (RELAY, -RELAY):
        pl.semaphore_signal(far_sem, inc=1, device_id=along_seq(offset), device_id_type=MESH)

    attend(qkv, 0, WIN)
    attend(qkv, 1, 2 * WIN)
    normed[0 : 3 * WIN] = project(3 * WIN, resid[0:3].reshape(3 * WIN, D))

    r = lax.broadcasted_iota(jnp.int32, (TOK * 8, 4 * WIN), 0)
    c = lax.broadcasted_iota(jnp.int32, (TOK * 8, 4 * WIN), 1)
    target = (me + place_offset(r // 8)) & (SEQ - 1)
    hit = (target == col_slot) & ((r & 3) == (c & 3))
    pick_low = (hit & ((r & 4) == 0)).astype(jnp.bfloat16)
    pick_high = (hit & ((r & 4) != 0)).astype(jnp.bfloat16)

    def picked(rows):
        low_half = jnp.dot(
            pick_low[:, rows], normed[rows, :HALF], preferred_element_type=jnp.float32
        )
        return low_half + jnp.dot(
            pick_high[:, rows], normed[rows, HALF:], preferred_element_type=jnp.float32
        )

    placed = picked(slice(0, 2 * WIN))
    lending.wait()
    placed = placed + picked(slice(2 * WIN, 4 * WIN))
    outgoing[...] = placed.astype(jnp.bfloat16).reshape(TOK, 8, HALF)

    own = pltpu.make_async_copy(outgoing.at[0], out_hbm.at[0], own_sem)
    own.start()

    pl.semaphore_wait(far_sem, 2)

    def token(place, device):
        return pltpu.make_async_remote_copy(
            src_ref=outgoing.at[pl.ds(place, 1)],
            dst_ref=out_hbm.at[pl.ds(place, 1)],
            send_sem=token_send.at[place],
            recv_sem=token_recv.at[place],
            device_id=device,
            device_id_type=MESH,
        )

    first_legs = []
    for leg, (place, count) in enumerate(RELAYED):
        first_legs.append(
            pltpu.make_async_remote_copy(
                src_ref=outgoing.at[pl.ds(place, count)],
                dst_ref=relay.at[pl.ds(2 * leg, count)],
                send_sem=relay_send.at[leg],
                recv_sem=relay_recv.at[leg],
                device_id=along_seq(RELAY),
                device_id_type=MESH,
            )
        )
        first_legs[-1].start()
    token(24, along_seq(32)).start()

    wrapping = jnp.clip(me - 40, 0, 23)
    low = jnp.clip(me - 8, 0, 20)

    def up(i):
        return jnp.where(i < wrapping, SEQ - me + i, jnp.minimum(SEQ - 1 - me, 23) - (i - wrapping))

    def down(i):
        return jnp.where(i < low, 8 + low - i, 28 - (i - low))

    @pl.loop(0, 20)
    def _(i):
        offset = down(i)
        token(18 + offset, along_seq(-offset)).start()

    for leg, (place, count) in enumerate(RELAYED):
        first_legs[leg].wait_recv()
        for q in range(count):
            held = 2 * leg + q
            pltpu.make_async_remote_copy(
                src_ref=relay.at[pl.ds(held, 1)],
                dst_ref=out_hbm.at[pl.ds(place + q, 1)],
                send_sem=token_send.at[place + q],
                recv_sem=token_recv.at[place + q],
                device_id=along_seq(33 + held - RELAY),
                device_id_type=MESH,
            ).start()

    @pl.loop(0, 23)
    def _(i):
        offset = up(i)
        token(offset, along_seq(offset)).start()

    own.wait()
    for leg in first_legs:
        leg.wait_send()

    @pl.loop(1, TOK)
    def _(place):
        token(place, along_seq(1)).wait()


def place_kernel(row_ref, arrived_ref, out_ref):
    me = lax.axis_index("seq")
    rows = TOK * 8
    g = lax.broadcasted_iota(jnp.int32, (SEQ, rows), 0)
    c = lax.broadcasted_iota(jnp.int32, (SEQ, rows), 1)
    sender = (me - place_offset(c // 8)) & (SEQ - 1)
    lm = jnp.broadcast_to(row_ref[...].astype(jnp.float32), (8, SEQ)).astype(jnp.bfloat16)
    row_of = jnp.dot(lm, (g == sender).astype(jnp.bfloat16), preferred_element_type=jnp.float32)
    row_of = row_of[0:1].astype(jnp.int32)
    r = lax.broadcasted_iota(jnp.int32, (TOK, rows), 0)
    c = lax.broadcasted_iota(jnp.int32, (TOK, rows), 1)
    hit = r == row_of
    arrived = arrived_ref[...].reshape(rows, HALF)
    pick = jnp.concatenate(
        [(hit & ((c & 7) == part)).astype(jnp.bfloat16) for part in range(8)], axis=0
    )
    cut = jnp.dot(pick, arrived, preferred_element_type=jnp.float32).astype(jnp.bfloat16)
    for part in range(8):
        at = part % 4 * D + part // 4 * HALF
        out_ref[:, at : at + HALF] = cut[TOK * part : TOK * (part + 1)]


def per_device(
    qkv, resid, block_count, send_count, send_slot, lm_row, out_weight, out_bias, norm_gain
):
    vmem = pl.BlockSpec(memory_space=pltpu.VMEM)
    smem = pl.BlockSpec(memory_space=pltpu.SMEM)
    hbm = pl.BlockSpec(memory_space=pl.ANY)
    dma = pltpu.SemaphoreType.DMA
    arrived = pl.pallas_call(
        encode_kernel,
        out_shape=pltpu.VMEM((TOK, 8, HALF), jnp.bfloat16),
        in_specs=[hbm, hbm, smem, smem, vmem, hbm, vmem, vmem],
        out_specs=vmem,
        scratch_shapes=[
            pltpu.VMEM((1,) + qkv.shape[1:], jnp.bfloat16),
            pltpu.VMEM((3,) + qkv.shape[1:], jnp.bfloat16),
            pltpu.VMEM(resid.shape, jnp.bfloat16),
            pltpu.VMEM((D, D), jnp.bfloat16),
            pltpu.VMEM((3 * WIN, D), jnp.bfloat16),
            pltpu.VMEM((WIN, D), jnp.bfloat16),
            pltpu.VMEM((4 * WIN, D), jnp.bfloat16),
            pltpu.VMEM((TOK, 8, HALF), jnp.bfloat16),
            pltpu.VMEM((3, 8, HALF), jnp.bfloat16),
            dma((4,)),
            dma((2,)),
            dma((2,)),
            dma((2,)),
            dma((TOK,)),
            dma((TOK,)),
            dma,
            pltpu.SemaphoreType.REGULAR,
            pltpu.SemaphoreType.REGULAR,
        ],
        compiler_params=pltpu.CompilerParams(collective_id=0, has_side_effects=True),
    )(
        qkv,
        resid,
        block_count,
        send_count,
        send_slot,
        out_weight,
        out_bias,
        norm_gain,
    )
    placed = pl.pallas_call(
        place_kernel,
        out_shape=jax.ShapeDtypeStruct((TOK, 4 * D), jnp.bfloat16),
        in_specs=[vmem, vmem],
        out_specs=vmem,
    )(lm_row, pltpu.with_memory_space_constraint(arrived, pltpu.VMEM))
    return placed[None]


def solution(mesh):
    placed = (
        P("enc", "seq", None),
        P("enc", "seq", None),
        P("enc", "seq"),
        P("enc", "seq"),
        P("enc", "seq"),
        P("enc", "seq"),
        P(),
        P(),
        P(),
    )
    return jax.shard_map(
        per_device, mesh=mesh, in_specs=placed, out_specs=P("enc", "seq", None), check_vma=False
    )
```

```python
import functools
import math

import jax
import jax.numpy as jnp
from jax import lax
from jax.experimental import pallas as pl
from jax.experimental.pallas import tpu as pltpu
from jax.sharding import PartitionSpec as P

MESH = pl.DeviceIdType.MESH
D = 1280
HALF = 640
HEAD = 80
WIN = 64
SEQ = 64
ENC = 16
TOK = 48
RELAY = 16
STEP = 8
NEAR = [d for d in range(-STEP, STEP + 1) if d]

RELAYED = ((25, 2), (47, 1))


def place_offset(place):
    return jnp.where(place < 24, place, jnp.where(place < 27, place + 8, 82 - place))


def encode_kernel(
    qkv_hbm,
    resid_hbm,
    count_ref,
    lent_ref,
    slot_ref,
    row_ref,
    weight_hbm,
    bias_ref,
    gain_ref,
    out_hbm,
    pick_ref,
    first_qkv,
    qkv,
    resid,
    weight,
    att,
    lend,
    normed,
    outgoing,
    relay,
    load_sem,
    lend_sem,
    relay_send,
    relay_recv,
    token_send,
    token_recv,
    own_sem,
    step_sem,
    far_sem,
):
    me = lax.axis_index("seq")
    enc = lax.axis_index("enc")

    def along_seq(offset):
        return (enc, lax.rem(me + offset + 2 * SEQ, SEQ))

    next_enc = (lax.rem(enc + 1, ENC), me)
    prev_enc = (lax.rem(enc + ENC - 1, ENC), me)

    barrier = pltpu.get_barrier_semaphore()
    for offset in NEAR:
        pl.semaphore_signal(barrier, inc=1, device_id=along_seq(offset), device_id_type=MESH)
    pl.semaphore_signal(barrier, inc=1, device_id=prev_enc, device_id_type=MESH)

    later = pl.ds(1, 3)
    top, bottom = pl.ds(0, HALF), pl.ds(HALF, HALF)
    loads = [
        pltpu.make_async_copy(qkv_hbm.at[later], qkv, load_sem.at[0]),
        pltpu.make_async_copy(weight_hbm.at[top], weight.at[top], load_sem.at[1]),
        pltpu.make_async_copy(weight_hbm.at[bottom], weight.at[bottom], load_sem.at[4]),
        pltpu.make_async_copy(resid_hbm, resid, load_sem.at[2]),
        pltpu.make_async_copy(qkv_hbm.at[pl.ds(0, 1)], first_qkv, load_sem.at[3]),
    ]
    for copy in loads:
        copy.start()

    live = count_ref[0, 0]
    kept = live - lent_ref[0, 0]
    last_live = jnp.clip(live - 1, 1, 3)
    bias = bias_ref[...].astype(jnp.float32).reshape(1, D)
    gain = gain_ref[...].astype(jnp.float32).reshape(1, D)

    col = lax.broadcasted_iota(jnp.int32, (1, 4 * WIN), 1)
    row48 = lax.broadcasted_iota(jnp.int32, (TOK, 4 * WIN), 0)
    col48 = lax.broadcasted_iota(jnp.int32, (TOK, 4 * WIN), 1)
    work_row = jnp.where(col48 < 3 * WIN, col48 // 4, (col48 - WIN) // 4)
    spread = (row48 == work_row).astype(jnp.bfloat16)
    slots = jnp.broadcast_to(slot_ref[...].astype(jnp.float32), (8, TOK)).astype(jnp.bfloat16)
    col_slot = jnp.dot(slots, spread, preferred_element_type=jnp.float32)[0:1].astype(jnp.int32)
    usable = jnp.where(col < 2 * WIN, 2, jnp.where(col < 3 * WIN, kept, 5 - kept)) >= jnp.where(
        col < 2 * WIN, 0, 3
    )
    col_slot = jnp.where(usable, col_slot, -1)

    half_scale = math.log2(math.e) / math.sqrt(HEAD)
    lane = lax.broadcasted_iota(jnp.int32, (1, 256), 1)
    head_mask = []
    ones_mask = []
    row128 = lax.broadcasted_iota(jnp.int32, (128, 256), 0)
    lane128 = lax.broadcasted_iota(jnp.int32, (128, 256), 1)
    for pair in range(4):
        low = 32 * pair
        first = ((lane >= low) & (lane < low + HEAD)).astype(jnp.bfloat16)
        second = ((lane >= low + HEAD) & (lane < low + 2 * HEAD)).astype(jnp.bfloat16)
        head_mask.append((first, second))
        start = jnp.where(row128 < WIN, low, low + HEAD)
        ones_mask.append(((lane128 >= start) & (lane128 < start + HEAD)).astype(jnp.bfloat16))
    left = lax.broadcasted_iota(jnp.int32, (WIN, 128), 1) < WIN

    def attend(qkv, slot, row):
        for group in range(2):
            num = [None] * 5
            den = [None] * 5
            for pair in range(4):
                at = HALF * group + 128 * pair
                q = qkv[slot, :, at : at + 256]
                k = qkv[slot, :, D + at : D + at + 256]
                v = qkv[slot, :, 2 * D + at : 2 * D + at + 256]
                first, second = head_mask[pair]
                keys = jnp.concatenate([k * first, k * second], axis=0)
                s = lax.dot_general(
                    q, keys, (((1,), (1,)), ((), ())), preferred_element_type=jnp.float32
                )
                top_a = jnp.max(jnp.where(left, s, -jnp.inf), axis=1, keepdims=True)
                top_b = jnp.max(jnp.where(left, -jnp.inf, s), axis=1, keepdims=True)
                p = jnp.exp2((s - jnp.where(left, top_a, top_b)) * half_scale).astype(jnp.bfloat16)
                values = jnp.concatenate([v * first, v * second], axis=0)
                o = jnp.dot(p, values, preferred_element_type=jnp.float32)
                total = jnp.dot(p, ones_mask[pair], preferred_element_type=jnp.float32)
                for part in range(2):
                    cut = slice(128 * part, 128 * part + 128)
                    tile = pair + part
                    num[tile] = o[:, cut] if num[tile] is None else num[tile] + o[:, cut]
                    den[tile] = total[:, cut] if den[tile] is None else den[tile] + total[:, cut]
            for tile in range(5):
                at = HALF * group + 128 * tile
                att[pl.ds(row, WIN), at : at + 128] = (num[tile] / den[tile]).astype(jnp.bfloat16)

    def project(hidden, resid_rows):
        hidden = hidden + bias + resid_rows.astype(jnp.float32)
        inv_rms = lax.rsqrt(jnp.mean(hidden * hidden, axis=-1, keepdims=True) + 1e-06)
        return (hidden * inv_rms * gain).astype(jnp.bfloat16)

    loads[0].wait()
    attend(qkv, last_live - 1, 0)
    pl.semaphore_wait(barrier, len(NEAR) + 1)
    for offset in (STEP, -STEP):
        pl.semaphore_signal(step_sem, inc=1, device_id=along_seq(offset), device_id_type=MESH)
    loads[1].wait()
    hidden = jnp.dot(att[0:WIN, :HALF], weight[:HALF], preferred_element_type=jnp.float32)
    loads[2].wait()
    loads[3].wait()
    hidden = hidden + jnp.dot(
        att[0:WIN, HALF:], weight[HALF:], preferred_element_type=jnp.float32
    )
    lend[...] = project(hidden, resid[last_live])

    lending = pltpu.make_async_remote_copy(
        src_ref=lend,
        dst_ref=normed.at[pl.ds(3 * WIN, WIN)],
        send_sem=lend_sem.at[0],
        recv_sem=lend_sem.at[1],
        device_id=next_enc,
        device_id_type=MESH,
    )
    lending.start()

    loads[4].wait()
    attend(first_qkv, 0, 0)
    pl.semaphore_wait(step_sem, 2)
    for offset in (RELAY, -RELAY):
        pl.semaphore_signal(far_sem, inc=1, device_id=along_seq(offset), device_id_type=MESH)

    attend(qkv, 0, WIN)
    attend(qkv, 1, 2 * WIN)
    hidden = jnp.dot(att[...], weight[...], preferred_element_type=jnp.float32)
    normed[0 : 3 * WIN] = project(hidden, resid[0:3].reshape(3 * WIN, D))

    r = lax.broadcasted_iota(jnp.int32, (TOK * 8, 4 * WIN), 0)
    c = lax.broadcasted_iota(jnp.int32, (TOK * 8, 4 * WIN), 1)
    target = (me + place_offset(r // 8)) & (SEQ - 1)
    hit = (target == col_slot) & ((r & 3) == (c & 3))
    pick_low = (hit & ((r & 4) == 0)).astype(jnp.bfloat16)
    pick_high = (hit & ((r & 4) != 0)).astype(jnp.bfloat16)

    def picked(places, rows):
        low_half = jnp.dot(
            pick_low[places, rows], normed[rows, :HALF], preferred_element_type=jnp.float32
        )
        return low_half + jnp.dot(
            pick_high[places, rows], normed[rows, HALF:], preferred_element_type=jnp.float32
        )

    near, far = slice(0, 4 * TOK), slice(4 * TOK, 8 * TOK)
    own, rest = slice(0, 2 * WIN), slice(2 * WIN, 4 * WIN)
    placed = picked(far, own)
    placed_near = picked(near, own)
    lending.wait()
    placed = placed + picked(far, rest)
    outgoing[TOK // 2 :] = placed.astype(jnp.bfloat16).reshape(TOK // 2, 8, HALF)

    pl.semaphore_wait(far_sem, 2)

    def token(place, device):
        return pltpu.make_async_remote_copy(
            src_ref=outgoing.at[pl.ds(place, 1)],
            dst_ref=out_hbm.at[pl.ds(place, 1)],
            send_sem=token_send.at[place],
            recv_sem=token_recv.at[place],
            device_id=device,
            device_id_type=MESH,
        )

    first_legs = []
    for leg, (place, count) in enumerate(RELAYED):
        first_legs.append(
            pltpu.make_async_remote_copy(
                src_ref=outgoing.at[pl.ds(place, count)],
                dst_ref=relay.at[pl.ds(2 * leg, count)],
                send_sem=relay_send.at[leg],
                recv_sem=relay_recv.at[leg],
                device_id=along_seq(RELAY),
                device_id_type=MESH,
            )
        )
        first_legs[-1].start()
    token(24, along_seq(32)).start()

    wrapping = jnp.clip(me - 40, 0, 23)
    low = jnp.clip(me - 8, 0, 20)

    def up(i):
        return jnp.where(i < wrapping, SEQ - me + i, jnp.minimum(SEQ - 1 - me, 23) - (i - wrapping))

    def down(i):
        return jnp.where(i < low, 8 + low - i, 28 - (i - low))

    @pl.loop(0, 20)
    def _(i):
        offset = down(i)
        token(18 + offset, along_seq(-offset)).start()

    placed_near = placed_near + picked(near, rest)
    outgoing[0 : TOK // 2] = placed_near.astype(jnp.bfloat16).reshape(TOK // 2, 8, HALF)

    for leg, (place, count) in enumerate(RELAYED):
        first_legs[leg].wait_recv()
        for q in range(count):
            held = 2 * leg + q
            pltpu.make_async_remote_copy(
                src_ref=relay.at[pl.ds(held, 1)],
                dst_ref=out_hbm.at[pl.ds(place + q, 1)],
                send_sem=token_send.at[place + q],
                recv_sem=token_recv.at[place + q],
                device_id=along_seq(33 + held - RELAY),
                device_id_type=MESH,
            ).start()

    @pl.loop(0, 23)
    def _(i):
        offset = up(i)
        token(offset, along_seq(offset)).start()

    own_copy = pltpu.make_async_copy(outgoing.at[0], out_hbm.at[0], own_sem)
    own_copy.start()

    rows = TOK * 8
    g = lax.broadcasted_iota(jnp.int32, (SEQ, rows), 0)
    c = lax.broadcasted_iota(jnp.int32, (SEQ, rows), 1)
    sender = (me - place_offset(c // 8)) & (SEQ - 1)
    lm = jnp.broadcast_to(row_ref[...].astype(jnp.float32), (8, SEQ)).astype(jnp.bfloat16)
    row_of = jnp.dot(lm, (g == sender).astype(jnp.bfloat16), preferred_element_type=jnp.float32)
    row_of = row_of[0:1].astype(jnp.int32)
    r = lax.broadcasted_iota(jnp.int32, (TOK, rows), 0)
    c = lax.broadcasted_iota(jnp.int32, (TOK, rows), 1)
    hit = r == row_of
    for part in range(8):
        pick_ref[TOK * part : TOK * (part + 1)] = (hit & ((c & 7) == part)).astype(jnp.bfloat16)

    own_copy.wait()
    for leg in first_legs:
        leg.wait_send()

    @pl.loop(1, TOK)
    def _(place):
        token(place, along_seq(1)).wait()


def place_kernel(pick_ref, arrived_ref, out_hbm, staged, sems):
    arrived = arrived_ref[...].reshape(TOK * 8, HALF)
    copies = []
    for half in range(2):
        rows = slice(4 * TOK * half, 4 * TOK * (half + 1))
        cut = jnp.dot(pick_ref[rows], arrived, preferred_element_type=jnp.float32)
        for patch in range(4):
            part = 4 * half + patch
            staged[part] = cut[TOK * patch : TOK * (patch + 1)].astype(jnp.bfloat16)
            at = patch * D + half * HALF
            copies.append(
                pltpu.make_async_copy(
                    staged.at[part], out_hbm.at[:, pl.ds(at, HALF)], sems.at[part]
                )
            )
            copies[-1].start()
    for copy in copies:
        copy.wait()


def per_device(
    qkv, resid, block_count, send_count, send_slot, lm_row, out_weight, out_bias, norm_gain
):
    vmem = pl.BlockSpec(memory_space=pltpu.VMEM)
    smem = pl.BlockSpec(memory_space=pltpu.SMEM)
    hbm = pl.BlockSpec(memory_space=pl.ANY)
    dma = pltpu.SemaphoreType.DMA
    arrived, pick = pl.pallas_call(
        encode_kernel,
        out_shape=(
            pltpu.VMEM((TOK, 8, HALF), jnp.bfloat16),
            pltpu.VMEM((TOK * 8, TOK * 8), jnp.bfloat16),
        ),
        in_specs=[hbm, hbm, smem, smem, vmem, vmem, hbm, vmem, vmem],
        out_specs=(vmem, vmem),
        scratch_shapes=[
            pltpu.VMEM((1,) + qkv.shape[1:], jnp.bfloat16),
            pltpu.VMEM((3,) + qkv.shape[1:], jnp.bfloat16),
            pltpu.VMEM(resid.shape, jnp.bfloat16),
            pltpu.VMEM((D, D), jnp.bfloat16),
            pltpu.VMEM((3 * WIN, D), jnp.bfloat16),
            pltpu.VMEM((WIN, D), jnp.bfloat16),
            pltpu.VMEM((4 * WIN, D), jnp.bfloat16),
            pltpu.VMEM((TOK, 8, HALF), jnp.bfloat16),
            pltpu.VMEM((3, 8, HALF), jnp.bfloat16),
            dma((5,)),
            dma((2,)),
            dma((2,)),
            dma((2,)),
            dma((TOK,)),
            dma((TOK,)),
            dma,
            pltpu.SemaphoreType.REGULAR,
            pltpu.SemaphoreType.REGULAR,
        ],
        compiler_params=pltpu.CompilerParams(collective_id=0, has_side_effects=True),
    )(
        qkv,
        resid,
        block_count,
        send_count,
        send_slot,
        lm_row,
        out_weight,
        out_bias,
        norm_gain,
    )
    placed = pl.pallas_call(
        place_kernel,
        out_shape=jax.ShapeDtypeStruct((TOK, 4 * D), jnp.bfloat16),
        in_specs=[vmem, vmem],
        out_specs=hbm,
        scratch_shapes=[pltpu.VMEM((8, TOK, HALF), jnp.bfloat16), dma((8,))],
    )(
        pltpu.with_memory_space_constraint(pick, pltpu.VMEM),
        pltpu.with_memory_space_constraint(arrived, pltpu.VMEM),
    )
    return placed[None]


def solution(mesh):
    placed = (
        P("enc", "seq", None),
        P("enc", "seq", None),
        P("enc", "seq"),
        P("enc", "seq"),
        P("enc", "seq"),
        P("enc", "seq"),
        P(),
        P(),
        P(),
    )
    return jax.shard_map(
        per_device, mesh=mesh, in_specs=placed, out_specs=P("enc", "seq", None), check_vma=False
    )
```

```python
import functools
import math

import jax
import jax.numpy as jnp
from jax import lax
from jax.experimental import pallas as pl
from jax.experimental.pallas import tpu as pltpu
from jax.sharding import PartitionSpec as P

MESH = pl.DeviceIdType.MESH
D = 1280
HALF = 640
HEAD = 80
WIN = 64
SEQ = 64
ENC = 16
TOK = 48
RELAY = 16
STEP = 8
NEAR = [d for d in range(-STEP, STEP + 1) if d]

RELAYED = ((25, 2), (47, 1))


def place_offset(place):
    return jnp.where(place < 24, place, jnp.where(place < 27, place + 8, 82 - place))


def encode_kernel(
    qkv_hbm,
    resid_hbm,
    count_ref,
    lent_ref,
    slot_ref,
    row_ref,
    weight_hbm,
    bias_ref,
    gain_ref,
    out_hbm,
    pick_ref,
    first_qkv,
    qkv,
    resid,
    weight,
    att,
    lend,
    normed,
    outgoing,
    relay,
    load_sem,
    lend_sem,
    relay_send,
    relay_recv,
    token_send,
    token_recv,
    own_sem,
    step_sem,
    far_sem,
):
    me = lax.axis_index("seq")
    enc = lax.axis_index("enc")

    def along_seq(offset):
        return (enc, lax.rem(me + offset + 2 * SEQ, SEQ))

    next_enc = (lax.rem(enc + 1, ENC), me)
    prev_enc = (lax.rem(enc + ENC - 1, ENC), me)

    barrier = pltpu.get_barrier_semaphore()
    for offset in NEAR:
        pl.semaphore_signal(barrier, inc=1, device_id=along_seq(offset), device_id_type=MESH)
    pl.semaphore_signal(barrier, inc=1, device_id=prev_enc, device_id_type=MESH)

    later = pl.ds(1, 3)
    top, bottom = pl.ds(0, HALF), pl.ds(HALF, HALF)
    loads = [
        pltpu.make_async_copy(qkv_hbm.at[later], qkv, load_sem.at[0]),
        pltpu.make_async_copy(weight_hbm.at[top], weight.at[top], load_sem.at[1]),
        pltpu.make_async_copy(weight_hbm.at[bottom], weight.at[bottom], load_sem.at[4]),
        pltpu.make_async_copy(resid_hbm, resid, load_sem.at[2]),
        pltpu.make_async_copy(qkv_hbm.at[pl.ds(0, 1)], first_qkv, load_sem.at[3]),
    ]
    for copy in loads:
        copy.start()

    live = count_ref[0, 0]
    kept = live - lent_ref[0, 0]
    last_live = jnp.clip(live - 1, 1, 3)
    bias = bias_ref[...].astype(jnp.float32).reshape(1, D)
    gain = gain_ref[...].astype(jnp.float32).reshape(1, D)

    col = lax.broadcasted_iota(jnp.int32, (1, 4 * WIN), 1)
    row48 = lax.broadcasted_iota(jnp.int32, (TOK, 4 * WIN), 0)
    col48 = lax.broadcasted_iota(jnp.int32, (TOK, 4 * WIN), 1)
    work_row = jnp.where(col48 < 3 * WIN, col48 // 4, (col48 - WIN) // 4)
    spread = (row48 == work_row).astype(jnp.bfloat16)
    slots = jnp.broadcast_to(slot_ref[...].astype(jnp.float32), (8, TOK)).astype(jnp.bfloat16)
    col_slot = jnp.dot(slots, spread, preferred_element_type=jnp.float32)[0:1].astype(jnp.int32)
    usable = jnp.where(col < 2 * WIN, 2, jnp.where(col < 3 * WIN, kept, 5 - kept)) >= jnp.where(
        col < 2 * WIN, 0, 3
    )
    col_slot = jnp.where(usable, col_slot, -1)

    half_scale = math.log2(math.e) / math.sqrt(HEAD)
    lane = lax.broadcasted_iota(jnp.int32, (1, 256), 1)
    head_mask = []
    ones_mask = []
    row128 = lax.broadcasted_iota(jnp.int32, (128, 256), 0)
    lane128 = lax.broadcasted_iota(jnp.int32, (128, 256), 1)
    for pair in range(4):
        low = 32 * pair
        first = ((lane >= low) & (lane < low + HEAD)).astype(jnp.bfloat16)
        second = ((lane >= low + HEAD) & (lane < low + 2 * HEAD)).astype(jnp.bfloat16)
        head_mask.append((first, second))
        start = jnp.where(row128 < WIN, low, low + HEAD)
        ones_mask.append(((lane128 >= start) & (lane128 < start + HEAD)).astype(jnp.bfloat16))
    left = lax.broadcasted_iota(jnp.int32, (WIN, 128), 1) < WIN

    def attend(qkv, slot, row):
        for group in range(2):
            num = [None] * 5
            den = [None] * 5
            for pair in range(4):
                at = HALF * group + 128 * pair
                q = qkv[slot, :, at : at + 256]
                k = qkv[slot, :, D + at : D + at + 256]
                v = qkv[slot, :, 2 * D + at : 2 * D + at + 256]
                first, second = head_mask[pair]
                keys = jnp.concatenate([k * first, k * second], axis=0)
                s = lax.dot_general(
                    q, keys, (((1,), (1,)), ((), ())), preferred_element_type=jnp.float32
                )
                top_a = jnp.max(jnp.where(left, s, -jnp.inf), axis=1, keepdims=True)
                top_b = jnp.max(jnp.where(left, -jnp.inf, s), axis=1, keepdims=True)
                p = jnp.exp2((s - jnp.where(left, top_a, top_b)) * half_scale).astype(jnp.bfloat16)
                values = jnp.concatenate([v * first, v * second], axis=0)
                o = jnp.dot(p, values, preferred_element_type=jnp.float32)
                total = jnp.dot(p, ones_mask[pair], preferred_element_type=jnp.float32)
                for part in range(2):
                    cut = slice(128 * part, 128 * part + 128)
                    tile = pair + part
                    num[tile] = o[:, cut] if num[tile] is None else num[tile] + o[:, cut]
                    den[tile] = total[:, cut] if den[tile] is None else den[tile] + total[:, cut]
            for tile in range(5):
                at = HALF * group + 128 * tile
                att[pl.ds(row, WIN), at : at + 128] = (num[tile] / den[tile]).astype(jnp.bfloat16)

    def project(hidden, resid_rows):
        hidden = hidden + bias + resid_rows.astype(jnp.float32)
        inv_rms = lax.rsqrt(jnp.mean(hidden * hidden, axis=-1, keepdims=True) + 1e-06)
        return (hidden * inv_rms * gain).astype(jnp.bfloat16)

    loads[0].wait()
    attend(qkv, last_live - 1, 0)
    pl.semaphore_wait(barrier, len(NEAR) + 1)
    for offset in (STEP, -STEP):
        pl.semaphore_signal(step_sem, inc=1, device_id=along_seq(offset), device_id_type=MESH)
    loads[1].wait()
    hidden = jnp.dot(att[0:WIN, :HALF], weight[:HALF], preferred_element_type=jnp.float32)
    loads[2].wait()
    loads[3].wait()
    hidden = hidden + jnp.dot(
        att[0:WIN, HALF:], weight[HALF:], preferred_element_type=jnp.float32
    )
    lend[...] = project(hidden, resid[last_live])

    lending = pltpu.make_async_remote_copy(
        src_ref=lend,
        dst_ref=normed.at[pl.ds(3 * WIN, WIN)],
        send_sem=lend_sem.at[0],
        recv_sem=lend_sem.at[1],
        device_id=next_enc,
        device_id_type=MESH,
    )
    lending.start()

    loads[4].wait()
    attend(first_qkv, 0, 0)
    pl.semaphore_wait(step_sem, 2)
    for offset in (RELAY, -RELAY):
        pl.semaphore_signal(far_sem, inc=1, device_id=along_seq(offset), device_id_type=MESH)

    attend(qkv, 0, WIN)
    attend(qkv, 1, 2 * WIN)
    hidden = jnp.dot(att[...], weight[...], preferred_element_type=jnp.float32)
    normed[0 : 3 * WIN] = project(hidden, resid[0:3].reshape(3 * WIN, D))

    r = lax.broadcasted_iota(jnp.int32, (TOK * 8, 4 * WIN), 0)
    c = lax.broadcasted_iota(jnp.int32, (TOK * 8, 4 * WIN), 1)
    target = (me + place_offset(r // 8)) & (SEQ - 1)
    hit = (target == col_slot) & ((r & 3) == (c & 3))
    pick_low = (hit & ((r & 4) == 0)).astype(jnp.bfloat16)
    pick_high = (hit & ((r & 4) != 0)).astype(jnp.bfloat16)

    def picked(places, rows):
        low_half = jnp.dot(
            pick_low[places, rows], normed[rows, :HALF], preferred_element_type=jnp.float32
        )
        return low_half + jnp.dot(
            pick_high[places, rows], normed[rows, HALF:], preferred_element_type=jnp.float32
        )

    near, far = slice(0, 4 * TOK), slice(4 * TOK, 8 * TOK)
    own, rest = slice(0, 2 * WIN), slice(2 * WIN, 4 * WIN)
    placed = picked(far, own)
    placed_near = picked(near, own)
    lending.wait()
    placed = placed + picked(far, rest)
    outgoing[TOK // 2 :] = placed.astype(jnp.bfloat16).reshape(TOK // 2, 8, HALF)

    pl.semaphore_wait(far_sem, 2)

    def token(place, device):
        return pltpu.make_async_remote_copy(
            src_ref=outgoing.at[pl.ds(place, 1)],
            dst_ref=out_hbm.at[pl.ds(place, 1)],
            send_sem=token_send.at[place],
            recv_sem=token_recv.at[place],
            device_id=device,
            device_id_type=MESH,
        )

    first_legs = []
    for leg, (place, count) in enumerate(RELAYED):
        first_legs.append(
            pltpu.make_async_remote_copy(
                src_ref=outgoing.at[pl.ds(place, count)],
                dst_ref=relay.at[pl.ds(2 * leg, count)],
                send_sem=relay_send.at[leg],
                recv_sem=relay_recv.at[leg],
                device_id=along_seq(RELAY),
                device_id_type=MESH,
            )
        )
        first_legs[-1].start()
    token(24, along_seq(32)).start()

    wrapping = jnp.clip(me - 40, 0, 23)
    low = jnp.clip(me - 8, 0, 20)

    def up(i):
        return jnp.where(i < wrapping, SEQ - me + i, jnp.minimum(SEQ - 1 - me, 23) - (i - wrapping))

    def down(i):
        return jnp.where(i < low, 8 + low - i, 28 - (i - low))

    @pl.loop(0, 20, unroll=True)
    def _(i):
        offset = down(i)
        token(18 + offset, along_seq(-offset)).start()

    placed_near = placed_near + picked(near, rest)
    outgoing[0 : TOK // 2] = placed_near.astype(jnp.bfloat16).reshape(TOK // 2, 8, HALF)

    for leg, (place, count) in enumerate(RELAYED):
        first_legs[leg].wait_recv()
        for q in range(count):
            held = 2 * leg + q
            pltpu.make_async_remote_copy(
                src_ref=relay.at[pl.ds(held, 1)],
                dst_ref=out_hbm.at[pl.ds(place + q, 1)],
                send_sem=token_send.at[place + q],
                recv_sem=token_recv.at[place + q],
                device_id=along_seq(33 + held - RELAY),
                device_id_type=MESH,
            ).start()

    @pl.loop(0, 23, unroll=True)
    def _(i):
        offset = up(i)
        token(offset, along_seq(offset)).start()

    own_copy = pltpu.make_async_copy(outgoing.at[0], out_hbm.at[0], own_sem)
    own_copy.start()

    rows = TOK * 8
    g = lax.broadcasted_iota(jnp.int32, (SEQ, rows), 0)
    c = lax.broadcasted_iota(jnp.int32, (SEQ, rows), 1)
    sender = (me - place_offset(c // 8)) & (SEQ - 1)
    lm = jnp.broadcast_to(row_ref[...].astype(jnp.float32), (8, SEQ)).astype(jnp.bfloat16)
    row_of = jnp.dot(lm, (g == sender).astype(jnp.bfloat16), preferred_element_type=jnp.float32)
    row_of = row_of[0:1].astype(jnp.int32)
    r = lax.broadcasted_iota(jnp.int32, (TOK, rows), 0)
    c = lax.broadcasted_iota(jnp.int32, (TOK, rows), 1)
    hit = r == row_of
    for part in range(8):
        pick_ref[TOK * part : TOK * (part + 1)] = (hit & ((c & 7) == part)).astype(jnp.bfloat16)

    own_copy.wait()
    for leg in first_legs:
        leg.wait_send()

    @pl.loop(1, TOK)
    def _(place):
        token(place, along_seq(1)).wait()


def place_kernel(pick_ref, arrived_ref, out_hbm, staged, sems):
    arrived = arrived_ref[...].reshape(TOK * 8, HALF)
    copies = []
    for half in range(2):
        rows = slice(4 * TOK * half, 4 * TOK * (half + 1))
        cut = jnp.dot(pick_ref[rows], arrived, preferred_element_type=jnp.float32)
        for patch in range(4):
            part = 4 * half + patch
            staged[part] = cut[TOK * patch : TOK * (patch + 1)].astype(jnp.bfloat16)
            at = patch * D + half * HALF
            copies.append(
                pltpu.make_async_copy(
                    staged.at[part], out_hbm.at[:, pl.ds(at, HALF)], sems.at[part]
                )
            )
            copies[-1].start()
    for copy in copies:
        copy.wait()


def per_device(
    qkv, resid, block_count, send_count, send_slot, lm_row, out_weight, out_bias, norm_gain
):
    vmem = pl.BlockSpec(memory_space=pltpu.VMEM)
    smem = pl.BlockSpec(memory_space=pltpu.SMEM)
    hbm = pl.BlockSpec(memory_space=pl.ANY)
    dma = pltpu.SemaphoreType.DMA
    arrived, pick = pl.pallas_call(
        encode_kernel,
        out_shape=(
            pltpu.VMEM((TOK, 8, HALF), jnp.bfloat16),
            pltpu.VMEM((TOK * 8, TOK * 8), jnp.bfloat16),
        ),
        in_specs=[hbm, hbm, smem, smem, vmem, vmem, hbm, vmem, vmem],
        out_specs=(vmem, vmem),
        scratch_shapes=[
            pltpu.VMEM((1,) + qkv.shape[1:], jnp.bfloat16),
            pltpu.VMEM((3,) + qkv.shape[1:], jnp.bfloat16),
            pltpu.VMEM(resid.shape, jnp.bfloat16),
            pltpu.VMEM((D, D), jnp.bfloat16),
            pltpu.VMEM((3 * WIN, D), jnp.bfloat16),
            pltpu.VMEM((WIN, D), jnp.bfloat16),
            pltpu.VMEM((4 * WIN, D), jnp.bfloat16),
            pltpu.VMEM((TOK, 8, HALF), jnp.bfloat16),
            pltpu.VMEM((3, 8, HALF), jnp.bfloat16),
            dma((5,)),
            dma((2,)),
            dma((2,)),
            dma((2,)),
            dma((TOK,)),
            dma((TOK,)),
            dma,
            pltpu.SemaphoreType.REGULAR,
            pltpu.SemaphoreType.REGULAR,
        ],
        compiler_params=pltpu.CompilerParams(collective_id=0, has_side_effects=True),
    )(
        qkv,
        resid,
        block_count,
        send_count,
        send_slot,
        lm_row,
        out_weight,
        out_bias,
        norm_gain,
    )
    placed = pl.pallas_call(
        place_kernel,
        out_shape=jax.ShapeDtypeStruct((TOK, 4 * D), jnp.bfloat16),
        in_specs=[vmem, vmem],
        out_specs=hbm,
        scratch_shapes=[pltpu.VMEM((8, TOK, HALF), jnp.bfloat16), dma((8,))],
    )(
        pltpu.with_memory_space_constraint(pick, pltpu.VMEM),
        pltpu.with_memory_space_constraint(arrived, pltpu.VMEM),
    )
    return placed[None]


def solution(mesh):
    placed = (
        P("enc", "seq", None),
        P("enc", "seq", None),
        P("enc", "seq"),
        P("enc", "seq"),
        P("enc", "seq"),
        P("enc", "seq"),
        P(),
        P(),
        P(),
    )
    return jax.shard_map(
        per_device, mesh=mesh, in_specs=placed, out_specs=P("enc", "seq", None), check_vma=False
    )
```
